32 devices in a mesh: groups: 2 (over y), ctx: 4 (over z), tp: 2 (over x), kv: 2 (over core).
Axes of the slice: x: 2, y: 2, z: 4, core: 2. Of those that a mesh axis runs over, the one named last changes fastest.
Arguments:
- queries: bfloat16 [2048, 8192], P(('groups', 'ctx'), ('tp', 'kv')), parts along dimension 0, may hold values from -8 to 8
- key_matrix: bfloat16 [2048, 1024], P(('groups', 'ctx'), 'tp'), parts along dimension 0, may hold values from -8 to 8
- value_matrix: bfloat16 [2048, 1024], P(('groups', 'ctx'), 'tp'), parts along dimension 0, may hold values from -6 to 6
- out_grad: bfloat16 [2048, 8192], P(('groups', 'ctx'), ('tp', 'kv')), parts along dimension 0, may hold values from -6 to 6
- segments: int32 [2048], P(('groups', 'ctx')), parts along dimension 0, may hold values from 0 to 15, never falling along the last dimension, each value on 1 to 512 neighbouring positions
Outputs:
- query_grad: bfloat16 [2048, 8192], P(('groups', 'ctx'), ('tp', 'kv')), parts along dimension 0
- key_gradient: bfloat16 [2048, 1024], P(('groups', 'ctx'), 'tp'), parts along dimension 0
- value_gradient: bfloat16 [2048, 1024], P(('groups', 'ctx'), 'tp'), parts along dimension 0
The draws below stay inside these ranges and needn't reach their ends.
There are 2 independent parts, one for each index of `groups`. The reference program is written for one: setup_inputs(seed, part) draws one part's arguments, and reference() takes and returns one part's arrays. A program takes and returns all parts, laid end to end along the dimension named above; each array names one. Nothing has to cross between parts.
Inputs may be any that keep to these rules, and one draw needn't show every extreme that they name: `segments`: document numbers never fall along the sequence; each of the 16 documents has 1 or more positions and one document holds exactly half of the 1024 positions.
All inputs are finite; a program needn't handle non-finite values.
Results may differ from the reference program's by a relative error of at most 0.011.
Values may be sent and summed in bfloat16 or wider, within the bound.
A program may use at most 64 MiB of HBM per device.

```python
import math
import jax
import jax.numpy as jnp
import numpy as np
from jax import lax

QUERY_HEADS = 64
KEY_VALUE_HEADS = 8
HEAD_SIZE = 128
DOCS = 16
PACKED_LENGTH = 1024


def draw_key_matrix(key, part):
    output_rows = jnp.clip(jax.random.normal(jax.random.fold_in(key, 11), (PACKED_LENGTH, KEY_VALUE_HEADS, HEAD_SIZE), jnp.float32), -6.0, 6.0)
    return output_rows.reshape(PACKED_LENGTH, KEY_VALUE_HEADS * HEAD_SIZE).astype(jnp.bfloat16)


def draw_queries(key, part):
    output_rows = jnp.clip(jax.random.normal(jax.random.fold_in(key, 13), (PACKED_LENGTH, QUERY_HEADS, HEAD_SIZE), jnp.float32), -6.0, 6.0)
    return output_rows.reshape(PACKED_LENGTH, QUERY_HEADS * HEAD_SIZE).astype(jnp.bfloat16)


def levels(rng, shape, split, least, top_value):
    level, own = 1.0, jax.random.fold_in(rng, 6)
    for dim, blocks in split:
        draws = jnp.exp(jax.random.uniform(jax.random.fold_in(own, dim), (blocks,), jnp.float32, least / len(split), top_value / len(split)))
        level = level * jnp.repeat(draws, shape[dim] // blocks).reshape([-1 if axis == dim else 1 for axis in range(len(shape))])
    return level


def split_up(number_of, total, bound, slope):
    loads = [(1 << 20) // math.isqrt(rank ** slope) + 1 for rank in range(2, number_of + 1)]
    spare, given = total - bound - (number_of - 1), [1] * (number_of - 1)
    while spare > 0:
        movable = [i for i in range(number_of - 1) if given[i] < bound]
        whole, budget = sum([loads[i] for i in movable]), spare
        for i in movable:
            addition = min(bound - given[i], max(1, budget * loads[i] // whole), spare)
            given[i] = given[i] + addition
            spare = spare - addition
    return np.array([bound] + given)


def ragged(rng, number_of, total, reach, lean):
    if number_of == 2:
        one = jax.random.randint(rng, (), max(1, total - reach), min(reach, total - 1) + 1)
        return jnp.stack([one, total - one])
    sizes = jnp.asarray(split_up(number_of, total, reach, lean), jnp.int32)
    couples = (number_of - 1) // 2
    giver, receiver = sizes[1:1 + 2 * couples:2], sizes[2:2 + 2 * couples:2]
    margin = jnp.minimum(giver - 1, reach - receiver)
    moved = jax.random.randint(jax.random.fold_in(rng, 1), (couples,), 0, 1 << 20) % (margin + 1)
    sizes = sizes.at[1:1 + 2 * couples:2].set(giver - moved).at[2:2 + 2 * couples:2].set(receiver + moved)
    return sizes[jax.random.permutation(jax.random.fold_in(rng, 2), number_of)]


def centred(rng, shape, width, bound, pieces=(), kind=jnp.bfloat16):
    array = jax.random.normal(rng, shape, jnp.float32) * width
    if len(pieces) > 0:
        array = levels(rng, shape, pieces, -0.22, 0.18) * array
    return jnp.clip(array, min=-bound, max=bound).astype(kind)


def setup_inputs(seed: int = 0, part: int = 0) -> dict:
    seeds = jax.random.split(jax.random.key(seed), 6)
    part_splits = jax.random.split(jax.random.fold_in(seeds[5], part), 6)
    queries = draw_queries(jax.random.fold_in(jax.random.fold_in(seeds[5], part), 71), part)
    key_matrix = draw_key_matrix(jax.random.fold_in(jax.random.fold_in(seeds[5], part), 71), part)
    value_matrix = centred(part_splits[2], (PACKED_LENGTH, KEY_VALUE_HEADS * HEAD_SIZE), 1.0, 6.0, ((0, 4), (1, 2)))
    out_grad = centred(part_splits[3], (PACKED_LENGTH, QUERY_HEADS * HEAD_SIZE), 1.0, 6.0, ((0, 4), (1, 4)))
    segments = jnp.searchsorted(jnp.cumsum(ragged(part_splits[4], DOCS, PACKED_LENGTH, PACKED_LENGTH // 2, 2)), jnp.arange(PACKED_LENGTH), side="right").astype(jnp.int32)
    return {"queries": queries, "key_matrix": key_matrix, "value_matrix": value_matrix, "out_grad": out_grad, "segments": segments}


def head_backward(inputs, segments, logit_scale):
    q_head, g_head, k_head, v_head = inputs
    span_length = q_head.shape[0]
    parts_count = 8
    rows_each = span_length // parts_count
    position = jnp.arange(span_length, dtype=jnp.int32)
    query_pieces = []
    key_total = jnp.zeros((span_length, HEAD_SIZE), jnp.float32)
    value_total = jnp.zeros((span_length, HEAD_SIZE), jnp.float32)
    for piece_index in range(parts_count):
        row_first = piece_index * rows_each
        row_end = row_first + rows_each
        q_rows = q_head[row_first:row_end]
        g_rows = g_head[row_first:row_end]
        k_rows = k_head[:row_end]
        v_rows = v_head[:row_end]
        allowed = (segments[row_first:row_end, None] == segments[None, :row_end]) & (position[None, :row_end] <= position[row_first:row_end, None])
        logits = jnp.dot(q_rows, k_rows.T, preferred_element_type=jnp.float32) * logit_scale
        masked_logits = jnp.where(allowed, logits, -jnp.inf)
        row_peak = jnp.max(masked_logits, axis=1, keepdims=True)
        totals = jnp.sum(jnp.where(allowed, jnp.exp(logits - row_peak), 0.0), axis=1, keepdims=True)
        log_total = row_peak + jnp.log(totals)
        probs = jnp.where(allowed, jnp.exp(logits - log_total), 0.0)
        dprobs = jnp.dot(g_rows, v_rows.T, preferred_element_type=jnp.float32)
        deltas = jnp.sum(probs * dprobs, axis=1, keepdims=True)
        dlogits = probs * (dprobs - deltas)
        probs_low = probs.astype(jnp.bfloat16)
        dlogits_low = dlogits.astype(jnp.bfloat16)
        query_pieces.append(jnp.dot(dlogits_low, k_rows, preferred_element_type=jnp.float32) * logit_scale)
        key_piece = jnp.dot(dlogits_low.T, q_rows, preferred_element_type=jnp.float32)
        value_piece = jnp.dot(probs_low.T, g_rows, preferred_element_type=jnp.float32)
        key_total = key_total + jnp.pad(key_piece, ((0, span_length - row_end), (0, 0)))
        value_total = value_total + jnp.pad(value_piece, ((0, span_length - row_end), (0, 0)))
    return jnp.concatenate(query_pieces, axis=0), key_total, value_total


def reference(queries, key_matrix, value_matrix, out_grad, segments):
    span_length = queries.shape[0]
    group_width = QUERY_HEADS // KEY_VALUE_HEADS
    logit_scale = HEAD_SIZE ** -0.5
    q_heads = queries.reshape(span_length, QUERY_HEADS, HEAD_SIZE).transpose(1, 0, 2)
    g_heads = out_grad.reshape(span_length, QUERY_HEADS, HEAD_SIZE).transpose(1, 0, 2)
    key_head_list = jnp.repeat(key_matrix.reshape(span_length, KEY_VALUE_HEADS, HEAD_SIZE).transpose(1, 0, 2), group_width, axis=0)
    value_head_list = jnp.repeat(value_matrix.reshape(span_length, KEY_VALUE_HEADS, HEAD_SIZE).transpose(1, 0, 2), group_width, axis=0)

    def one_head(inputs):
        return head_backward(inputs, segments, logit_scale)

    query_parts, key_portions, value_portions = lax.map(one_head, (q_heads, g_heads, key_head_list, value_head_list))
    query_grad = query_parts.transpose(1, 0, 2).reshape(span_length, QUERY_HEADS * HEAD_SIZE).astype(jnp.bfloat16)
    key_total_sum = jnp.sum(key_portions.reshape(KEY_VALUE_HEADS, group_width, span_length, HEAD_SIZE), axis=1) * logit_scale
    value_total_sum = jnp.sum(value_portions.reshape(KEY_VALUE_HEADS, group_width, span_length, HEAD_SIZE), axis=1)
    key_gradient = key_total_sum.transpose(1, 0, 2).reshape(span_length, KEY_VALUE_HEADS * HEAD_SIZE).astype(jnp.bfloat16)
    value_gradient = value_total_sum.transpose(1, 0, 2).reshape(span_length, KEY_VALUE_HEADS * HEAD_SIZE).astype(jnp.bfloat16)
    return query_grad, key_gradient, value_gradient
```

```python
import functools
import jax
import jax.numpy as jnp
from jax import lax
from jax.experimental import pallas as pl
from jax.experimental.pallas import tpu as pltpu
from jax.sharding import PartitionSpec as P

QUERY_HEADS = 64
KEY_VALUE_HEADS = 8
HEAD_SIZE = 128
HALF = 128
LOG2E = 1.4426950408889634
NEG = -1e30
MESH = pl.DeviceIdType.MESH
NT = (((1,), (1,)), ((), ()))


def kernel(
    n, reach, rows, per_kv, kv_count, shared,
    q_hbm, k_hbm, v_hbm, g_hbm, seg_ref,
    dq_hbm, dk_hbm, dv_hbm,
    qv, gv, dqv, win, segwin, segcol, bias, kt, acc, sendb, ret, fin, pfin,
    load_sem, own_sem, seg_send, seg_recv, send_sem, recv_sem, back_send, back_recv,
    pair_send, pair_recv, dq_sem, out_sem,
):
    rank = lax.axis_index("ctx")
    kv = lax.axis_index("kv")
    up = lax.rem(rank + 1, n)
    down = lax.rem(rank + n - 1, n)
    mate = 1 - kv
    scale = HEAD_SIZE ** -0.5
    width = reach * rows + HALF
    halves = rows // HALF
    first = 0 if shared else kv * kv_count
    mate_first = 0 if shared else mate * kv_count

    def cols(base, g):
        if shared:
            return pl.ds(g * HEAD_SIZE, HEAD_SIZE)
        return pl.ds(pl.multiple_of((base + g) * HEAD_SIZE, HEAD_SIZE), HEAD_SIZE)

    def slot(d):
        return pl.ds((reach - d) * rows, rows)

    loads = [
        pltpu.make_async_copy(q_hbm, qv, load_sem.at[0]),
        pltpu.make_async_copy(g_hbm, gv, load_sem.at[1]),
    ]
    owns = []
    for g in range(kv_count):
        for t, ref in ((0, k_hbm), (1, v_hbm)):
            owns.append(
                pltpu.make_async_copy(
                    ref.at[:, cols(first, g)], win.at[t, g, slot(0)], own_sem.at[t, g]
                )
            )

    def forward(t, g, d):
        ref = k_hbm if t == 0 else v_hbm
        src = ref.at[:, cols(first, g)] if d == 0 else win.at[t, g, slot(d)]
        return pltpu.make_async_remote_copy(
            src_ref=src,
            dst_ref=win.at[t, g, slot(d + 1)],
            send_sem=send_sem.at[t, g, d],
            recv_sem=recv_sem.at[t, g, d + 1],
            device_id={"ctx": up},
            device_id_type=MESH,
        )

    def forward_seg(d):
        return pltpu.make_async_remote_copy(
            src_ref=seg_ref if d == 0 else segwin.at[d],
            dst_ref=segwin.at[d + 1],
            send_sem=seg_send.at[d],
            recv_sem=seg_recv.at[d + 1],
            device_id={"ctx": up},
            device_id_type=MESH,
        )

    def back(g, d):
        return pltpu.make_async_remote_copy(
            src_ref=sendb.at[g, d - 1],
            dst_ref=ret.at[g, d - 1],
            send_sem=back_send.at[g, d - 1],
            recv_sem=back_recv.at[g, d - 1],
            device_id={"ctx": down},
            device_id_type=MESH,
        )

    def to_mate(g):
        return pltpu.make_async_remote_copy(
            src_ref=fin.at[g],
            dst_ref=pfin.at[g],
            send_sem=pair_send.at[g],
            recv_sem=pair_recv.at[g],
            device_id={"kv": mate},
            device_id_type=MESH,
        )

    has_up = rank < n - 1

    for copy in loads + owns:
        copy.start()

    barrier = pltpu.get_barrier_semaphore()
    pl.semaphore_signal(barrier, inc=1, device_id={"kv": mate}, device_id_type=MESH)

    @pl.when(has_up)
    def _():
        pl.semaphore_signal(barrier, inc=1, device_id={"ctx": up}, device_id_type=MESH)

    @pl.when(rank > 0)
    def _():
        pl.semaphore_signal(barrier, inc=1, device_id={"ctx": down}, device_id_type=MESH)

    expected = 1 + jnp.where(has_up, 1, 0) + jnp.where(rank > 0, 1, 0)
    pl.semaphore_wait(barrier, expected)

    @pl.when(has_up)
    def _():
        forward_seg(0).start()
        forward(0, 0, 0).start()
        forward(1, 0, 0).start()

    for d in range(1, reach + 1):
        @pl.when(rank < d)
        def _(d=d):
            for g in range(kv_count):
                for t in range(2):
                    win[t, g, slot(d), :] = jnp.zeros((rows, HEAD_SIZE), jnp.bfloat16)
            segwin[d] = jnp.full((1, rows), -1, jnp.int32)

    acc[...] = jnp.zeros_like(acc)

    def pass_on_seg():
        for d in range(1, reach + 1):
            @pl.when(rank >= d)
            def _(d=d):
                forward_seg(d - 1).wait_recv()

            if d < reach:
                @pl.when((rank >= d) & has_up)
                def _(d=d):
                    forward_seg(d).start()

    def pass_on(g):
        for d in range(1, reach):
            for t in range(2):
                @pl.when(rank >= d)
                def _(d=d, t=t):
                    forward(t, g, d - 1).wait_recv()

                @pl.when((rank >= d) & has_up)
                def _(d=d, t=t):
                    forward(t, g, d).start()

    def last_slot(g):
        @pl.when(rank >= reach)
        def _():
            for t in range(2):
                forward(t, g, reach - 1).wait_recv()

    def send_own(g):
        @pl.when(has_up)
        def _():
            for t in range(2):
                forward(t, g, 0).start()

    def make_bias():
        for d in range(reach + 1):
            row = (seg_ref[...] if d == 0 else segwin[d]).astype(jnp.float32)
            segcol[slot(d), :] = jnp.broadcast_to(row, (HALF, rows)).T
        key_at = lax.broadcasted_iota(jnp.int32, (width, HALF), 0)
        query_at = lax.broadcasted_iota(jnp.int32, (width, HALF), 1)
        causal = key_at <= query_at + reach * rows
        for h in range(halves):
            seg_q = seg_ref[:, h * HALF:(h + 1) * HALF].astype(jnp.float32)
            same = segcol[h * HALF:h * HALF + width, :] == seg_q
            bias[h] = jnp.where(same & causal, 0.0, NEG)

    def unit(g, h, p):
        span = slice(h * HALF, h * HALF + width)
        part = slice(h * HALF, (h + 1) * HALF)
        c0 = pl.multiple_of((g * per_kv + 2 * p) * HEAD_SIZE, HEAD_SIZE)
        c1 = pl.multiple_of((g * per_kv + 2 * p + 1) * HEAD_SIZE, HEAD_SIZE)
        one, two = pl.ds(c0, HEAD_SIZE), pl.ds(c1, HEAD_SIZE)
        qu = jnp.concatenate([qv[part, one], qv[part, two]], axis=0)
        gu = jnp.concatenate([gv[part, one], gv[part, two]], axis=0)
        s = lax.dot_general(win[0, g, span, :], qu, NT, preferred_element_type=jnp.float32)
        dp = lax.dot_general(win[1, g, span, :], gu, NT, preferred_element_type=jnp.float32)
        b = bias[h]
        s = s + jnp.concatenate([b, b], axis=1)
        peak = jnp.max(s, axis=0, keepdims=True)
        e = jnp.exp2((s - peak) * (scale * LOG2E))
        inv = 1.0 / jnp.sum(e, axis=0, keepdims=True)
        delta = jnp.sum(e * dp, axis=0, keepdims=True) * inv
        pn = e * inv
        ds = (pn * (dp - delta)).astype(jnp.bfloat16)
        pb = pn.astype(jnp.bfloat16)
        dqt = jnp.dot(kt[g, :, span], ds, preferred_element_type=jnp.float32)
        dq = (dqt * scale).T.astype(jnp.bfloat16)
        dqv[part, one] = dq[:HALF]
        dqv[part, two] = dq[HALF:]
        acc[g, 0, span, :] += jnp.dot(ds, qu, preferred_element_type=jnp.float32)
        acc[g, 1, span, :] += jnp.dot(pb, gu, preferred_element_type=jnp.float32)

    def units(g, begin, end):
        def body(p, carry):
            for h in range(halves):
                unit(g, h, p)
            return carry

        lax.fori_loop(begin, end, body, 0)

    def send_back(g, d):
        if d < reach:
            @pl.when(has_up & (rank >= d))
            def _():
                back(g, d + 1).wait_recv()
                sendb[g, d - 1] = (
                    acc[g, :, slot(d), :] + ret[g, d].astype(jnp.float32)
                ).astype(jnp.bfloat16)

            @pl.when(jnp.logical_not(has_up) & (rank >= d))
            def _():
                sendb[g, d - 1] = acc[g, :, slot(d), :].astype(jnp.bfloat16)
        else:
            @pl.when(rank >= d)
            def _():
                sendb[g, d - 1] = acc[g, :, slot(d), :].astype(jnp.bfloat16)

        @pl.when(rank >= d)
        def _():
            back(g, d).start()

    def finish(g):
        @pl.when(has_up)
        def _():
            back(g, 1).wait_recv()
            for t in range(2):
                acc[g, t, slot(0), :] += ret[g, 0, t].astype(jnp.float32)

        for t in range(2):
            factor = scale if t == 0 else 1.0
            fin[g, t] = (acc[g, t, slot(0), :] * factor).astype(jnp.bfloat16)
        to_mate(g).start()

    pass_on_seg()
    make_bias()
    pass_on(0)
    for copy in loads + owns:
        copy.wait()
    split = per_kv // 4
    for g in range(kv_count):
        if g + 1 < kv_count:
            send_own(g + 1)
        last_slot(g)
        kt[g] = win[0, g].T
        units(g, 0, split)
        if g + 1 < kv_count:
            pass_on(g + 1)
        if g > 0:
            for d in range(reach - 1, 0, -1):
                send_back(g - 1, d)
        units(g, split, per_kv // 2)
        send_back(g, reach)
        wide = pl.ds(g * per_kv * HEAD_SIZE, per_kv * HEAD_SIZE)
        pltpu.make_async_copy(dqv.at[:, wide], dq_hbm.at[:, wide], dq_sem.at[g]).start()
    for d in range(reach - 1, 0, -1):
        send_back(kv_count - 1, d)
    for g in range(kv_count):
        finish(g)

    outs = []
    for g in range(kv_count):
        to_mate(g).wait()
        if shared:
            for t in range(2):
                pfin[g, t] = (
                    fin[g, t].astype(jnp.float32) + pfin[g, t].astype(jnp.float32)
                ).astype(jnp.bfloat16)
        for t, ref in ((0, dk_hbm), (1, dv_hbm)):
            outs.append(
                pltpu.make_async_copy(
                    pfin.at[g, t], ref.at[:, cols(mate_first, g)], out_sem.at[0, t, g]
                )
            )
            if not shared:
                outs.append(
                    pltpu.make_async_copy(
                        fin.at[g, t], ref.at[:, cols(first, g)], out_sem.at[1, t, g]
                    )
                )
                outs[-1].start()
                outs[-2].start()
            else:
                outs[-1].start()
    for g in range(kv_count):
        wide = pl.ds(g * per_kv * HEAD_SIZE, per_kv * HEAD_SIZE)
        pltpu.make_async_copy(dqv.at[:, wide], dq_hbm.at[:, wide], dq_sem.at[g]).wait()
    for copy in outs:
        copy.wait()
    for d in range(reach):
        @pl.when(has_up & (rank >= d))
        def _(d=d):
            forward_seg(d).wait_send()
            for g in range(kv_count):
                for t in range(2):
                    forward(t, g, d).wait_send()
    for d in range(1, reach + 1):
        @pl.when(rank >= d)
        def _(d=d):
            for g in range(kv_count):
                back(g, d).wait_send()


def shards(queries, key_matrix, value_matrix, out_grad, segments):
    n = lax.axis_size("ctx")
    rows = queries.shape[0]
    head_count = queries.shape[1] // HEAD_SIZE
    group_width = QUERY_HEADS // KEY_VALUE_HEADS
    kv_count = max(head_count // group_width, 1)
    per_kv = head_count // kv_count
    kv_here = key_matrix.shape[1] // HEAD_SIZE
    shared = kv_here < kv_count * lax.axis_size("kv")
    reach = n // 2
    window = (reach + 1) * rows
    width = reach * rows + HALF
    bf16, f32 = jnp.bfloat16, jnp.float32
    dma = pltpu.SemaphoreType.DMA
    anywhere = pl.BlockSpec(memory_space=pl.ANY)
    return pl.pallas_call(
        functools.partial(kernel, n, reach, rows, per_kv, kv_count, shared),
        out_shape=(
            jax.ShapeDtypeStruct(queries.shape, bf16),
            jax.ShapeDtypeStruct(key_matrix.shape, bf16),
            jax.ShapeDtypeStruct(value_matrix.shape, bf16),
        ),
        in_specs=[anywhere] * 4 + [pl.BlockSpec(memory_space=pltpu.VMEM)],
        out_specs=(anywhere,) * 3,
        scratch_shapes=[
            pltpu.VMEM(queries.shape, bf16),
            pltpu.VMEM(queries.shape, bf16),
            pltpu.VMEM(queries.shape, bf16),
            pltpu.VMEM((2, kv_count, window, HEAD_SIZE), bf16),
            pltpu.VMEM((reach + 1, 1, rows), jnp.int32),
            pltpu.VMEM((window, HALF), f32),
            pltpu.VMEM((rows // HALF, width, HALF), f32),
            pltpu.VMEM((kv_count, HEAD_SIZE, window), bf16),
            pltpu.VMEM((kv_count, 2, window, HEAD_SIZE), f32),
            pltpu.VMEM((kv_count, reach, 2, rows, HEAD_SIZE), bf16),
            pltpu.VMEM((kv_count, reach, 2, rows, HEAD_SIZE), bf16),
            pltpu.VMEM((kv_count, 2, rows, HEAD_SIZE), bf16),
            pltpu.VMEM((kv_count, 2, rows, HEAD_SIZE), bf16),
            dma((2,)),
            dma((2, kv_count)),
            dma((reach + 1,)),
            dma((reach + 1,)),
            dma((2, kv_count, reach + 1)),
            dma((2, kv_count, reach + 1)),
            dma((kv_count, reach)),
            dma((kv_count, reach)),
            dma((kv_count,)),
            dma((kv_count,)),
            dma((kv_count,)),
            dma((2, 2, kv_count)),
        ],
        compiler_params=pltpu.CompilerParams(
            collective_id=0, has_side_effects=True, vmem_limit_bytes=60 * 1024 * 1024
        ),
    )(queries, key_matrix, value_matrix, out_grad, segments.reshape(1, rows))


def solution(mesh):
    return jax.shard_map(
        shards,
        mesh=mesh,
        in_specs=(
            P(("groups", "ctx"), ("tp", "kv")),
            P(("groups", "ctx"), "tp"),
            P(("groups", "ctx"), "tp"),
            P(("groups", "ctx"), ("tp", "kv")),
            P(("groups", "ctx")),
        ),
        out_specs=(
            P(("groups", "ctx"), ("tp", "kv")),
            P(("groups", "ctx"), "tp"),
            P(("groups", "ctx"), "tp"),
        ),
        check_vma=False,
    )
```

```python
import functools
import jax
import jax.numpy as jnp
from jax import lax
from jax.experimental import pallas as pl
from jax.experimental.pallas import tpu as pltpu
from jax.sharding import PartitionSpec as P

QUERY_HEADS = 64
KEY_VALUE_HEADS = 8
HEAD_SIZE = 128
HALF = 128
CHUNK = 32
LOG2E = 1.4426950408889634
NEG = -1e30
MESH = pl.DeviceIdType.MESH
NT = (((1,), (1,)), ((), ()))


def kernel(
    n, reach, rows, per_kv, kv_count, shared,
    q_hbm, k_hbm, v_hbm, g_hbm, seg_hbm,
    dqv, fin, other,
    qv, gv, sv, dpv, peaks, pv, dsv, win, segwin, segcol, bias, kt, acc, sendb, ret, pfin,
    load_sem, own_sem, seg_send, seg_recv, send_sem, recv_sem, back_send, back_recv,
    pair_send, pair_recv,
):
    rank = lax.axis_index("ctx")
    kv = lax.axis_index("kv")
    up = lax.rem(rank + 1, n)
    down = lax.rem(rank + n - 1, n)
    mate = 1 - kv
    scale = HEAD_SIZE ** -0.5
    width = reach * rows + HALF
    halves = rows // HALF
    first = 0 if shared else kv * kv_count

    def cols(base, g):
        if shared:
            return pl.ds(g * HEAD_SIZE, HEAD_SIZE)
        return pl.ds(pl.multiple_of((base + g) * HEAD_SIZE, HEAD_SIZE), HEAD_SIZE)

    def slot(d):
        return pl.ds((reach - d) * rows, rows)

    loads = [
        pltpu.make_async_copy(q_hbm, qv, load_sem.at[0]),
        pltpu.make_async_copy(g_hbm, gv, load_sem.at[1]),
    ]
    seg_load = pltpu.make_async_copy(seg_hbm, segwin.at[0], load_sem.at[2])
    owns = []
    for g in range(kv_count):
        for t, ref in ((0, k_hbm), (1, v_hbm)):
            owns.append(
                pltpu.make_async_copy(
                    ref.at[:, cols(first, g)], win.at[t, g, slot(0)], own_sem.at[t, g]
                )
            )

    def forward(t, g, d):
        ref = k_hbm if t == 0 else v_hbm
        src = ref.at[:, cols(first, g)] if d == 0 else win.at[t, g, slot(d)]
        return pltpu.make_async_remote_copy(
            src_ref=src,
            dst_ref=win.at[t, g, slot(d + 1)],
            send_sem=send_sem.at[t, g, d],
            recv_sem=recv_sem.at[t, g, d + 1],
            device_id={"ctx": up},
            device_id_type=MESH,
        )

    def forward_seg(d):
        return pltpu.make_async_remote_copy(
            src_ref=seg_hbm if d == 0 else segwin.at[d],
            dst_ref=segwin.at[d + 1],
            send_sem=seg_send.at[d],
            recv_sem=seg_recv.at[d + 1],
            device_id={"ctx": up},
            device_id_type=MESH,
        )

    def back(g, d):
        return pltpu.make_async_remote_copy(
            src_ref=sendb.at[g, d - 1],
            dst_ref=ret.at[g, d - 1],
            send_sem=back_send.at[g, d - 1],
            recv_sem=back_recv.at[g, d - 1],
            device_id={"ctx": down},
            device_id_type=MESH,
        )

    def to_mate(g):
        return pltpu.make_async_remote_copy(
            src_ref=fin.at[g],
            dst_ref=pfin.at[g],
            send_sem=pair_send.at[g],
            recv_sem=pair_recv.at[g],
            device_id={"kv": mate},
            device_id_type=MESH,
        )

    has_up = rank < n - 1

    for copy in [seg_load] + owns + loads:
        copy.start()

    barrier = pltpu.get_barrier_semaphore()
    pl.semaphore_signal(barrier, inc=1, device_id={"kv": mate}, device_id_type=MESH)

    @pl.when(has_up)
    def _():
        pl.semaphore_signal(barrier, inc=1, device_id={"ctx": up}, device_id_type=MESH)

    @pl.when(rank > 0)
    def _():
        pl.semaphore_signal(barrier, inc=1, device_id={"ctx": down}, device_id_type=MESH)

    expected = 1 + jnp.where(has_up, 1, 0) + jnp.where(rank > 0, 1, 0)
    pl.semaphore_wait(barrier, expected)

    @pl.when(has_up)
    def _():
        forward_seg(0).start()
        forward(0, 0, 0).start()
        forward(1, 0, 0).start()

    for d in range(1, reach + 1):
        @pl.when(rank < d)
        def _(d=d):
            for g in range(kv_count):
                for t in range(2):
                    win[t, g, slot(d), :] = jnp.zeros((rows, HEAD_SIZE), jnp.bfloat16)
            segwin[d] = jnp.full((1, rows), -1, jnp.int32)

    acc[...] = jnp.zeros_like(acc)

    def pass_on_seg():
        for d in range(1, reach + 1):
            @pl.when(rank >= d)
            def _(d=d):
                forward_seg(d - 1).wait_recv()

            if d < reach:
                @pl.when((rank >= d) & has_up)
                def _(d=d):
                    forward_seg(d).start()

    def pass_on(g):
        for d in range(1, reach):
            for t in range(2):
                @pl.when(rank >= d)
                def _(d=d, t=t):
                    forward(t, g, d - 1).wait_recv()

                @pl.when((rank >= d) & has_up)
                def _(d=d, t=t):
                    forward(t, g, d).start()

    def last_slot(g):
        @pl.when(rank >= reach)
        def _():
            for t in range(2):
                forward(t, g, reach - 1).wait_recv()

    def send_own(g):
        @pl.when(has_up)
        def _():
            for t in range(2):
                forward(t, g, 0).start()

    def make_bias():
        for d in range(reach + 1):
            row = segwin[d].astype(jnp.float32)
            segcol[slot(d), :] = jnp.broadcast_to(row, (HALF, rows)).T
        key_at = lax.broadcasted_iota(jnp.int32, (width, HALF), 0)
        query_at = lax.broadcasted_iota(jnp.int32, (width, HALF), 1)
        causal = key_at <= query_at + reach * rows
        for h in range(halves):
            seg_q = segwin[0, :, h * HALF:(h + 1) * HALF].astype(jnp.float32)
            same = segcol[h * HALF:h * HALF + width, :] == seg_q
            bias[h] = jnp.where(same & causal, 0.0, NEG)

    def spot(g, h, p):
        c0 = pl.multiple_of((g * per_kv + 2 * p) * HEAD_SIZE, HEAD_SIZE)
        c1 = pl.multiple_of((g * per_kv + 2 * p + 1) * HEAD_SIZE, HEAD_SIZE)
        part = slice(h * HALF, (h + 1) * HALF)
        return part, pl.ds(c0, HEAD_SIZE), pl.ds(c1, HEAD_SIZE)

    def pair(ref, g, h, p):
        part, one, two = spot(g, h, p)
        return jnp.concatenate([ref[part, one], ref[part, two]], axis=0)

    def span(h):
        return slice(h * HALF, h * HALF + width)

    def products(g, h, p):
        s = lax.dot_general(
            win[0, g, span(h), :], pair(qv, g, h, p), NT, preferred_element_type=jnp.float32
        )
        b = bias[h]
        s = s + jnp.concatenate([b, b], axis=1)
        sv[h] = s
        peaks[h] = jnp.max(s, axis=0, keepdims=True)
        dpv[h] = lax.dot_general(
            win[1, g, span(h), :], pair(gv, g, h, p), NT, preferred_element_type=jnp.float32
        )

    def softmax(h):
        peak = peaks[h]
        total = jnp.zeros((8, 2 * HALF), jnp.float32)
        weighted = jnp.zeros((8, 2 * HALF), jnp.float32)
        for c in range(0, width, CHUNK):
            rows_c = slice(c, c + CHUNK)
            e = jnp.exp2((sv[h, rows_c, :] - peak) * (scale * LOG2E))
            sv[h, rows_c, :] = e
            total = total + jnp.sum(e.reshape(-1, 8, 2 * HALF), axis=0)
            weighted = weighted + jnp.sum(
                (e * dpv[h, rows_c, :]).reshape(-1, 8, 2 * HALF), axis=0
            )
        inv = 1.0 / jnp.sum(total, axis=0, keepdims=True)
        delta = jnp.sum(weighted, axis=0, keepdims=True) * inv
        for c in range(0, width, CHUNK):
            rows_c = slice(c, c + CHUNK)
            pn = sv[h, rows_c, :] * inv
            dsv[h, rows_c, :] = (pn * (dpv[h, rows_c, :] - delta)).astype(jnp.bfloat16)
            pv[h, rows_c, :] = pn.astype(jnp.bfloat16)

    def grads(g, h, p):
        part, one, two = spot(g, h, p)
        ds = dsv[h]
        dqt = jnp.dot(kt[g, :, span(h)], ds, preferred_element_type=jnp.float32)
        dq = (dqt * scale).T.astype(jnp.bfloat16)
        dqv[part, one] = dq[:HALF]
        dqv[part, two] = dq[HALF:]
        acc[g, 0, span(h), :] += jnp.dot(
            ds, pair(qv, g, h, p), preferred_element_type=jnp.float32
        )
        acc[g, 1, span(h), :] += jnp.dot(
            pv[h], pair(gv, g, h, p), preferred_element_type=jnp.float32
        )

    pairs = per_kv // 2
    last_half = halves - 1

    def begin_units(g):
        dsv[last_half] = jnp.zeros((width, 2 * HALF), jnp.bfloat16)
        pv[last_half] = jnp.zeros((width, 2 * HALF), jnp.bfloat16)
        products(g, 0, 0)

    def units(g, begin, end):
        def body(p, carry):
            for h in range(halves):
                if h < last_half:
                    products(g, h + 1, p)
                else:
                    products(g, 0, jnp.minimum(p + 1, pairs - 1))
                softmax(h)
                if h > 0:
                    grads(g, h - 1, p)
                else:
                    grads(g, last_half, jnp.maximum(p - 1, 0))
            return carry

        lax.fori_loop(begin, end, body, 0)

    def end_units(g):
        grads(g, last_half, pairs - 1)

    def send_back(g, d):
        if d < reach:
            @pl.when(has_up & (rank >= d))
            def _():
                back(g, d + 1).wait_recv()
                sendb[g, d - 1] = (
                    acc[g, :, slot(d), :] + ret[g, d].astype(jnp.float32)
                ).astype(jnp.bfloat16)

            @pl.when(jnp.logical_not(has_up) & (rank >= d))
            def _():
                sendb[g, d - 1] = acc[g, :, slot(d), :].astype(jnp.bfloat16)
        else:
            @pl.when(rank >= d)
            def _():
                sendb[g, d - 1] = acc[g, :, slot(d), :].astype(jnp.bfloat16)

        @pl.when(rank >= d)
        def _():
            back(g, d).start()

    def finish(g):
        @pl.when(has_up)
        def _():
            back(g, 1).wait_recv()
            for t in range(2):
                acc[g, t, slot(0), :] += ret[g, 0, t].astype(jnp.float32)

        for t in range(2):
            factor = scale if t == 0 else 1.0
            fin[g, t] = (acc[g, t, slot(0), :] * factor).astype(jnp.bfloat16)
        to_mate(g).start()

    pass_on_seg()
    seg_load.wait()
    make_bias()
    pass_on(0)
    for copy in loads + owns:
        copy.wait()
    split = per_kv // 4
    for g in range(kv_count):
        if g + 1 < kv_count:
            send_own(g + 1)
        last_slot(g)
        kt[g] = win[0, g].T
        begin_units(g)
        units(g, 0, split)
        if g + 1 < kv_count:
            pass_on(g + 1)
        if g > 0:
            for d in range(reach - 1, 0, -1):
                send_back(g - 1, d)
        units(g, split, pairs)
        end_units(g)
        send_back(g, reach)
    for d in range(reach - 1, 0, -1):
        send_back(kv_count - 1, d)
    for g in range(kv_count):
        finish(g)

    for g in range(kv_count):
        to_mate(g).wait()
        for t in range(2):
            if shared:
                other[g, t] = (
                    fin[g, t].astype(jnp.float32) + pfin[g, t].astype(jnp.float32)
                ).astype(jnp.bfloat16)
            else:
                other[g, t] = pfin[g, t]
    for d in range(reach):
        @pl.when(has_up & (rank >= d))
        def _(d=d):
            forward_seg(d).wait_send()
            for g in range(kv_count):
                for t in range(2):
                    forward(t, g, d).wait_send()
    for d in range(1, reach + 1):
        @pl.when(rank >= d)
        def _(d=d):
            for g in range(kv_count):
                back(g, d).wait_send()


def place(kv_count, shared, dqv, fin, other, dq_hbm, dk_hbm, dv_hbm, sem):
    kv = lax.axis_index("kv")
    copies = [pltpu.make_async_copy(dqv, dq_hbm, sem.at[0])]
    parts = [(other, 0)] if shared else [(fin, kv * kv_count), (other, (1 - kv) * kv_count)]
    for source, base in parts:
        for g in range(kv_count):
            start = g * HEAD_SIZE
            if not shared:
                start = pl.multiple_of((base + g) * HEAD_SIZE, HEAD_SIZE)
            for t, ref in ((0, dk_hbm), (1, dv_hbm)):
                copies.append(
                    pltpu.make_async_copy(
                        source.at[g, t], ref.at[:, pl.ds(start, HEAD_SIZE)], sem.at[len(copies)]
                    )
                )
    for copy in copies:
        copy.start()
    for copy in copies:
        copy.wait()


def shards(queries, key_matrix, value_matrix, out_grad, segments):
    n = lax.axis_size("ctx")
    rows = queries.shape[0]
    head_count = queries.shape[1] // HEAD_SIZE
    group_width = QUERY_HEADS // KEY_VALUE_HEADS
    kv_count = max(head_count // group_width, 1)
    per_kv = head_count // kv_count
    kv_here = key_matrix.shape[1] // HEAD_SIZE
    shared = kv_here < kv_count * lax.axis_size("kv")
    reach = n // 2
    window = (reach + 1) * rows
    width = reach * rows + HALF
    halves = rows // HALF
    bf16, f32 = jnp.bfloat16, jnp.float32
    dma = pltpu.SemaphoreType.DMA
    anywhere = pl.BlockSpec(memory_space=pltpu.HBM)
    inner = pltpu.VMEM
    dqv, fin, other = pl.pallas_call(
        functools.partial(kernel, n, reach, rows, per_kv, kv_count, shared),
        out_shape=(
            inner(queries.shape, bf16),
            inner((kv_count, 2, rows, HEAD_SIZE), bf16),
            inner((kv_count, 2, rows, HEAD_SIZE), bf16),
        ),
        in_specs=[anywhere] * 5,
        out_specs=(pl.BlockSpec(memory_space=pltpu.VMEM),) * 3,
        scratch_shapes=[
            pltpu.VMEM(queries.shape, bf16),
            pltpu.VMEM(queries.shape, bf16),
            pltpu.VMEM((halves, width, 2 * HALF), f32),
            pltpu.VMEM((halves, width, 2 * HALF), f32),
            pltpu.VMEM((halves, 1, 2 * HALF), f32),
            pltpu.VMEM((halves, width, 2 * HALF), bf16),
            pltpu.VMEM((halves, width, 2 * HALF), bf16),
            pltpu.VMEM((2, kv_count, window, HEAD_SIZE), bf16),
            pltpu.VMEM((reach + 1, 1, rows), jnp.int32),
            pltpu.VMEM((window, HALF), f32),
            pltpu.VMEM((halves, width, HALF), f32),
            pltpu.VMEM((kv_count, HEAD_SIZE, window), bf16),
            pltpu.VMEM((kv_count, 2, window, HEAD_SIZE), f32),
            pltpu.VMEM((kv_count, reach, 2, rows, HEAD_SIZE), bf16),
            pltpu.VMEM((kv_count, reach, 2, rows, HEAD_SIZE), bf16),
            pltpu.VMEM((kv_count, 2, rows, HEAD_SIZE), bf16),
            dma((3,)),
            dma((2, kv_count)),
            dma((reach + 1,)),
            dma((reach + 1,)),
            dma((2, kv_count, reach + 1)),
            dma((2, kv_count, reach + 1)),
            dma((kv_count, reach)),
            dma((kv_count, reach)),
            dma((kv_count,)),
            dma((kv_count,)),
        ],
        compiler_params=pltpu.CompilerParams(
            collective_id=0, has_side_effects=True, vmem_limit_bytes=56 * 1024 * 1024
        ),
    )(queries, key_matrix, value_matrix, out_grad, segments.reshape(1, rows))
    return pl.pallas_call(
        functools.partial(place, kv_count, shared),
        out_shape=(
            jax.ShapeDtypeStruct(queries.shape, bf16),
            jax.ShapeDtypeStruct(key_matrix.shape, bf16),
            jax.ShapeDtypeStruct(value_matrix.shape, bf16),
        ),
        in_specs=[pl.BlockSpec(memory_space=pltpu.VMEM)] * 3,
        out_specs=(anywhere,) * 3,
        scratch_shapes=[dma((1 + 4 * kv_count,))],
        compiler_params=pltpu.CompilerParams(vmem_limit_bytes=4 * 1024 * 1024),
    )(dqv, fin, other)


def solution(mesh):
    return jax.shard_map(
        shards,
        mesh=mesh,
        in_specs=(
            P(("groups", "ctx"), ("tp", "kv")),
            P(("groups", "ctx"), "tp"),
            P(("groups", "ctx"), "tp"),
            P(("groups", "ctx"), ("tp", "kv")),
            P(("groups", "ctx")),
        ),
        out_specs=(
            P(("groups", "ctx"), ("tp", "kv")),
            P(("groups", "ctx"), "tp"),
            P(("groups", "ctx"), "tp"),
        ),
        check_vma=False,
    )
```

```python
import functools
import jax
import jax.numpy as jnp
from jax import lax
from jax.experimental import pallas as pl
from jax.experimental.pallas import tpu as pltpu
from jax.sharding import PartitionSpec as P

QUERY_HEADS = 64
KEY_VALUE_HEADS = 8
HEAD_SIZE = 128
HALF = 128
CHUNK = 32
LOG2E = 1.4426950408889634
NEG = -1e30
MESH = pl.DeviceIdType.MESH
NT = (((1,), (1,)), ((), ()))


def kernel(
    n, reach, rows, per_kv, kv_count, shared,
    q_hbm, k_hbm, v_hbm, g_hbm, seg_hbm,
    dqv, fin, other,
    qv, gv, sv, dpv, peaks, pv, dsv, win, segwin, segcol, bias, kt, acc, sendb, ret, pfin,
    load_sem, own_sem, seg_send, seg_recv, send_sem, recv_sem, back_send, back_recv,
    pair_send, pair_recv,
):
    rank = lax.axis_index("ctx")
    kv = lax.axis_index("kv")
    up = lax.rem(rank + 1, n)
    down = lax.rem(rank + n - 1, n)
    mate = 1 - kv
    scale = HEAD_SIZE ** -0.5
    width = reach * rows + HALF
    halves = rows // HALF
    first = 0 if shared else kv * kv_count

    def cols(base, g):
        if shared:
            return pl.ds(g * HEAD_SIZE, HEAD_SIZE)
        return pl.ds(pl.multiple_of((base + g) * HEAD_SIZE, HEAD_SIZE), HEAD_SIZE)

    def slot(d):
        return pl.ds((reach - d) * rows, rows)

    loads = [
        pltpu.make_async_copy(q_hbm, qv, load_sem.at[0]),
        pltpu.make_async_copy(g_hbm, gv, load_sem.at[1]),
    ]
    seg_load = pltpu.make_async_copy(seg_hbm, segwin.at[0], load_sem.at[2])
    owns = []
    for g in range(kv_count):
        for t, ref in ((0, k_hbm), (1, v_hbm)):
            owns.append(
                pltpu.make_async_copy(
                    ref.at[:, cols(first, g)], win.at[t, g, slot(0)], own_sem.at[t, g]
                )
            )

    def forward(t, g, d):
        ref = k_hbm if t == 0 else v_hbm
        src = ref.at[:, cols(first, g)] if d == 0 else win.at[t, g, slot(d)]
        return pltpu.make_async_remote_copy(
            src_ref=src,
            dst_ref=win.at[t, g, slot(d + 1)],
            send_sem=send_sem.at[t, g, d],
            recv_sem=recv_sem.at[t, g, d + 1],
            device_id={"ctx": up},
            device_id_type=MESH,
        )

    def forward_seg(d):
        return pltpu.make_async_remote_copy(
            src_ref=seg_hbm if d == 0 else segwin.at[d],
            dst_ref=segwin.at[d + 1],
            send_sem=seg_send.at[d],
            recv_sem=seg_recv.at[d + 1],
            device_id={"ctx": up},
            device_id_type=MESH,
        )

    def back(g, d, t):
        return pltpu.make_async_remote_copy(
            src_ref=sendb.at[g, d - 1, t],
            dst_ref=ret.at[g, d - 1, t],
            send_sem=back_send.at[g, d - 1, t],
            recv_sem=back_recv.at[g, d - 1, t],
            device_id={"ctx": down},
            device_id_type=MESH,
        )

    def to_mate(g, t):
        return pltpu.make_async_remote_copy(
            src_ref=fin.at[g, t],
            dst_ref=pfin.at[g, t],
            send_sem=pair_send.at[g, t],
            recv_sem=pair_recv.at[g, t],
            device_id={"kv": mate},
            device_id_type=MESH,
        )

    has_up = rank < n - 1

    for copy in [seg_load] + owns + loads:
        copy.start()

    barrier = pltpu.get_barrier_semaphore()
    pl.semaphore_signal(barrier, inc=1, device_id={"kv": mate}, device_id_type=MESH)

    @pl.when(has_up)
    def _():
        pl.semaphore_signal(barrier, inc=1, device_id={"ctx": up}, device_id_type=MESH)

    @pl.when(rank > 0)
    def _():
        pl.semaphore_signal(barrier, inc=1, device_id={"ctx": down}, device_id_type=MESH)

    expected = 1 + jnp.where(has_up, 1, 0) + jnp.where(rank > 0, 1, 0)
    pl.semaphore_wait(barrier, expected)

    @pl.when(has_up)
    def _():
        forward_seg(0).start()
        forward(0, 0, 0).start()
        forward(1, 0, 0).start()

    for d in range(1, reach + 1):
        @pl.when(rank < d)
        def _(d=d):
            for g in range(kv_count):
                for t in range(2):
                    win[t, g, slot(d), :] = jnp.zeros((rows, HEAD_SIZE), jnp.bfloat16)
            segwin[d] = jnp.full((1, rows), -1, jnp.int32)

    acc[...] = jnp.zeros_like(acc)

    def pass_on_seg():
        for d in range(1, reach + 1):
            @pl.when(rank >= d)
            def _(d=d):
                forward_seg(d - 1).wait_recv()

            if d < reach:
                @pl.when((rank >= d) & has_up)
                def _(d=d):
                    forward_seg(d).start()

    def pass_on(g):
        for d in range(1, reach):
            for t in range(2):
                @pl.when(rank >= d)
                def _(d=d, t=t):
                    forward(t, g, d - 1).wait_recv()

                @pl.when((rank >= d) & has_up)
                def _(d=d, t=t):
                    forward(t, g, d).start()

    def last_slot(g):
        @pl.when(rank >= reach)
        def _():
            for t in range(2):
                forward(t, g, reach - 1).wait_recv()

    def send_own(g):
        @pl.when(has_up)
        def _():
            for t in range(2):
                forward(t, g, 0).start()

    def make_bias():
        for d in range(reach + 1):
            row = segwin[d].astype(jnp.float32)
            segcol[slot(d), :] = jnp.broadcast_to(row, (HALF, rows)).T
        key_at = lax.broadcasted_iota(jnp.int32, (width, HALF), 0)
        query_at = lax.broadcasted_iota(jnp.int32, (width, HALF), 1)
        causal = key_at <= query_at + reach * rows
        for h in range(halves):
            seg_q = segwin[0, :, h * HALF:(h + 1) * HALF].astype(jnp.float32)
            same = segcol[h * HALF:h * HALF + width, :] == seg_q
            bias[h] = jnp.where(same & causal, 0.0, NEG)

    def spot(g, h, p):
        c0 = pl.multiple_of((g * per_kv + 2 * p) * HEAD_SIZE, HEAD_SIZE)
        c1 = pl.multiple_of((g * per_kv + 2 * p + 1) * HEAD_SIZE, HEAD_SIZE)
        part = slice(h * HALF, (h + 1) * HALF)
        return part, pl.ds(c0, HEAD_SIZE), pl.ds(c1, HEAD_SIZE)

    def pair(ref, g, h, p):
        part, one, two = spot(g, h, p)
        return jnp.concatenate([ref[part, one], ref[part, two]], axis=0)

    def span(h):
        return slice(h * HALF, h * HALF + width)

    def products(g, h, p):
        s = lax.dot_general(
            win[0, g, span(h), :], pair(qv, g, h, p), NT, preferred_element_type=jnp.float32
        )
        b = bias[h]
        s = s + jnp.concatenate([b, b], axis=1)
        sv[h] = s
        peaks[h] = jnp.max(s, axis=0, keepdims=True)
        dpv[h] = lax.dot_general(
            win[1, g, span(h), :], pair(gv, g, h, p), NT, preferred_element_type=jnp.float32
        )

    def softmax(h):
        peak = peaks[h]
        total = jnp.zeros((8, 2 * HALF), jnp.float32)
        weighted = jnp.zeros((8, 2 * HALF), jnp.float32)
        for c in range(0, width, CHUNK):
            rows_c = slice(c, c + CHUNK)
            e = jnp.exp2((sv[h, rows_c, :] - peak) * (scale * LOG2E))
            sv[h, rows_c, :] = e
            total = total + jnp.sum(e.reshape(-1, 8, 2 * HALF), axis=0)
            weighted = weighted + jnp.sum(
                (e * dpv[h, rows_c, :]).reshape(-1, 8, 2 * HALF), axis=0
            )
        inv = 1.0 / jnp.sum(total, axis=0, keepdims=True)
        delta = jnp.sum(weighted, axis=0, keepdims=True) * inv
        for c in range(0, width, CHUNK):
            rows_c = slice(c, c + CHUNK)
            pn = sv[h, rows_c, :] * inv
            dsv[h, rows_c, :] = (pn * (dpv[h, rows_c, :] - delta)).astype(jnp.bfloat16)
            pv[h, rows_c, :] = pn.astype(jnp.bfloat16)

    def grads(g, h, p):
        part, one, two = spot(g, h, p)
        ds = dsv[h]
        dqt = jnp.dot(kt[g, :, span(h)], ds, preferred_element_type=jnp.float32)
        dq = (dqt * scale).T.astype(jnp.bfloat16)
        dqv[part, one] = dq[:HALF]
        dqv[part, two] = dq[HALF:]
        acc[g, 0, span(h), :] += jnp.dot(
            ds, pair(qv, g, h, p), preferred_element_type=jnp.float32
        )
        acc[g, 1, span(h), :] += jnp.dot(
            pv[h], pair(gv, g, h, p), preferred_element_type=jnp.float32
        )

    pairs = per_kv // 2
    last_half = halves - 1

    def begin_units(g):
        dsv[last_half] = jnp.zeros((width, 2 * HALF), jnp.bfloat16)
        pv[last_half] = jnp.zeros((width, 2 * HALF), jnp.bfloat16)
        products(g, 0, 0)

    def units(g, begin, end):
        def body(p, carry):
            for h in range(halves):
                if h < last_half:
                    products(g, h + 1, p)
                else:
                    products(g, 0, jnp.minimum(p + 1, pairs - 1))
                softmax(h)
                if h > 0:
                    grads(g, h - 1, p)
                else:
                    grads(g, last_half, jnp.maximum(p - 1, 0))
            return carry

        lax.fori_loop(begin, end, body, 0)

    def end_units(g):
        grads(g, last_half, pairs - 1)

    def send_first(g):
        for d in range(reach, 0, -1):
            @pl.when((rank >= d) if d == reach else jnp.logical_not(has_up))
            def _(d=d):
                for t in range(2):
                    sendb[g, d - 1, t] = acc[g, t, slot(d), :].astype(jnp.bfloat16)
                    back(g, d, t).start()

    def send_rest(g):
        for d in range(reach - 1, 0, -1):
            @pl.when(has_up & (rank >= d))
            def _(d=d):
                for t in range(2):
                    back(g, d + 1, t).wait_recv()
                    sendb[g, d - 1, t] = (
                        acc[g, t, slot(d), :] + ret[g, d, t].astype(jnp.float32)
                    ).astype(jnp.bfloat16)
                    back(g, d, t).start()

    def finish(g):
        for t in range(2):
            @pl.when(has_up)
            def _(t=t):
                back(g, 1, t).wait_recv()
                acc[g, t, slot(0), :] += ret[g, 0, t].astype(jnp.float32)

            factor = scale if t == 0 else 1.0
            fin[g, t] = (acc[g, t, slot(0), :] * factor).astype(jnp.bfloat16)
            to_mate(g, t).start()

    pass_on_seg()
    seg_load.wait()
    make_bias()
    pass_on(0)
    for copy in loads + owns:
        copy.wait()
    middle, late = pairs // 2, pairs * 3 // 4
    for g in range(kv_count):
        if g + 1 < kv_count:
            send_own(g + 1)
        last_slot(g)
        kt[g] = win[0, g].T
        begin_units(g)
        if g + 1 < kv_count:
            units(g, 0, middle)
            pass_on(g + 1)
            units(g, middle, pairs)
        elif g > 0:
            units(g, 0, late)
            send_rest(g - 1)
            units(g, late, pairs)
        else:
            units(g, 0, pairs)
        end_units(g)
        send_first(g)
    send_rest(kv_count - 1)
    for g in range(kv_count):
        finish(g)

    for g in range(kv_count):
        for t in range(2):
            to_mate(g, t).wait()
            if shared:
                other[g, t] = (
                    fin[g, t].astype(jnp.float32) + pfin[g, t].astype(jnp.float32)
                ).astype(jnp.bfloat16)
            else:
                other[g, t] = pfin[g, t]
    for d in range(reach):
        @pl.when(has_up & (rank >= d))
        def _(d=d):
            forward_seg(d).wait_send()
            for g in range(kv_count):
                for t in range(2):
                    forward(t, g, d).wait_send()
    for d in range(1, reach + 1):
        @pl.when(rank >= d)
        def _(d=d):
            for g in range(kv_count):
                for t in range(2):
                    back(g, d, t).wait_send()


def place(kv_count, shared, dqv, fin, other, dq_hbm, dk_hbm, dv_hbm, sem):
    kv = lax.axis_index("kv")
    copies = [pltpu.make_async_copy(dqv, dq_hbm, sem.at[0])]
    parts = [(other, 0)] if shared else [(fin, kv * kv_count), (other, (1 - kv) * kv_count)]
    for source, base in parts:
        for g in range(kv_count):
            start = g * HEAD_SIZE
            if not shared:
                start = pl.multiple_of((base + g) * HEAD_SIZE, HEAD_SIZE)
            for t, ref in ((0, dk_hbm), (1, dv_hbm)):
                copies.append(
                    pltpu.make_async_copy(
                        source.at[g, t], ref.at[:, pl.ds(start, HEAD_SIZE)], sem.at[len(copies)]
                    )
                )
    for copy in copies:
        copy.start()
    for copy in copies:
        copy.wait()


def shards(queries, key_matrix, value_matrix, out_grad, segments):
    n = lax.axis_size("ctx")
    rows = queries.shape[0]
    head_count = queries.shape[1] // HEAD_SIZE
    group_width = QUERY_HEADS // KEY_VALUE_HEADS
    kv_count = max(head_count // group_width, 1)
    per_kv = head_count // kv_count
    kv_here = key_matrix.shape[1] // HEAD_SIZE
    shared = kv_here < kv_count * lax.axis_size("kv")
    reach = n // 2
    window = (reach + 1) * rows
    width = reach * rows + HALF
    halves = rows // HALF
    bf16, f32 = jnp.bfloat16, jnp.float32
    dma = pltpu.SemaphoreType.DMA
    anywhere = pl.BlockSpec(memory_space=pltpu.HBM)
    inner = pltpu.VMEM
    dqv, fin, other = pl.pallas_call(
        functools.partial(kernel, n, reach, rows, per_kv, kv_count, shared),
        out_shape=(
            inner(queries.shape, bf16),
            inner((kv_count, 2, rows, HEAD_SIZE), bf16),
            inner((kv_count, 2, rows, HEAD_SIZE), bf16),
        ),
        in_specs=[anywhere] * 5,
        out_specs=(pl.BlockSpec(memory_space=pltpu.VMEM),) * 3,
        scratch_shapes=[
            pltpu.VMEM(queries.shape, bf16),
            pltpu.VMEM(queries.shape, bf16),
            pltpu.VMEM((halves, width, 2 * HALF), f32),
            pltpu.VMEM((halves, width, 2 * HALF), f32),
            pltpu.VMEM((halves, 1, 2 * HALF), f32),
            pltpu.VMEM((halves, width, 2 * HALF), bf16),
            pltpu.VMEM((halves, width, 2 * HALF), bf16),
            pltpu.VMEM((2, kv_count, window, HEAD_SIZE), bf16),
            pltpu.VMEM((reach + 1, 1, rows), jnp.int32),
            pltpu.VMEM((window, HALF), f32),
            pltpu.VMEM((halves, width, HALF), f32),
            pltpu.VMEM((kv_count, HEAD_SIZE, window), bf16),
            pltpu.VMEM((kv_count, 2, window, HEAD_SIZE), f32),
            pltpu.VMEM((kv_count, reach, 2, rows, HEAD_SIZE), bf16),
            pltpu.VMEM((kv_count, reach, 2, rows, HEAD_SIZE), bf16),
            pltpu.VMEM((kv_count, 2, rows, HEAD_SIZE), bf16),
            dma((3,)),
            dma((2, kv_count)),
            dma((reach + 1,)),
            dma((reach + 1,)),
            dma((2, kv_count, reach + 1)),
            dma((2, kv_count, reach + 1)),
            dma((kv_count, reach, 2)),
            dma((kv_count, reach, 2)),
            dma((kv_count, 2)),
            dma((kv_count, 2)),
        ],
        compiler_params=pltpu.CompilerParams(
            collective_id=0, has_side_effects=True, vmem_limit_bytes=56 * 1024 * 1024
        ),
    )(queries, key_matrix, value_matrix, out_grad, segments.reshape(1, rows))
    return pl.pallas_call(
        functools.partial(place, kv_count, shared),
        out_shape=(
            jax.ShapeDtypeStruct(queries.shape, bf16),
            jax.ShapeDtypeStruct(key_matrix.shape, bf16),
            jax.ShapeDtypeStruct(value_matrix.shape, bf16),
        ),
        in_specs=[pl.BlockSpec(memory_space=pltpu.VMEM)] * 3,
        out_specs=(anywhere,) * 3,
        scratch_shapes=[dma((1 + 4 * kv_count,))],
        compiler_params=pltpu.CompilerParams(vmem_limit_bytes=4 * 1024 * 1024),
    )(dqv, fin, other)


def solution(mesh):
    return jax.shard_map(
        shards,
        mesh=mesh,
        in_specs=(
            P(("groups", "ctx"), ("tp", "kv")),
            P(("groups", "ctx"), "tp"),
            P(("groups", "ctx"), "tp"),
            P(("groups", "ctx"), ("tp", "kv")),
            P(("groups", "ctx")),
        ),
        out_specs=(
            P(("groups", "ctx"), ("tp", "kv")),
            P(("groups", "ctx"), "tp"),
            P(("groups", "ctx"), "tp"),
        ),
        check_vma=False,
    )
```

```python
import functools
import jax
import jax.numpy as jnp
from jax import lax
from jax.experimental import pallas as pl
from jax.experimental.pallas import tpu as pltpu
from jax.sharding import PartitionSpec as P

QUERY_HEADS = 64
KEY_VALUE_HEADS = 8
HEAD_SIZE = 128
HALF = 128
CHUNK = 32
LOG2E = 1.4426950408889634
NEG = -1e30
MESH = pl.DeviceIdType.MESH
NT = (((1,), (1,)), ((), ()))


def kernel(
    n, reach, rows, per_kv, kv_count, shared,
    q_hbm, k_hbm, v_hbm, g_hbm, seg_hbm,
    dqv, fin, other,
    qv, gv, sv, dpv, peaks, pv, dsv, win, segwin, segcol, bias, kt, acc, sendb, ret, pfin,
    load_sem, own_sem, seg_send, seg_recv, send_sem, recv_sem, back_send, back_recv,
    pair_send, pair_recv,
):
    rank = lax.axis_index("ctx")
    kv = lax.axis_index("kv")
    up = lax.rem(rank + 1, n)
    down = lax.rem(rank + n - 1, n)
    mate = 1 - kv
    scale = HEAD_SIZE ** -0.5
    width = reach * rows + HALF
    halves = rows // HALF
    first = 0 if shared else kv * kv_count

    def cols(base, g):
        if shared:
            return pl.ds(g * HEAD_SIZE, HEAD_SIZE)
        return pl.ds(pl.multiple_of((base + g) * HEAD_SIZE, HEAD_SIZE), HEAD_SIZE)

    def slot(d):
        return pl.ds((reach - d) * rows, rows)

    loads = [
        pltpu.make_async_copy(q_hbm, qv, load_sem.at[0]),
        pltpu.make_async_copy(g_hbm, gv, load_sem.at[1]),
    ]
    seg_load = pltpu.make_async_copy(seg_hbm, segwin.at[0], load_sem.at[2])
    owns = []
    for g in range(kv_count):
        for t, ref in ((0, k_hbm), (1, v_hbm)):
            owns.append(
                pltpu.make_async_copy(
                    ref.at[:, cols(first, g)], win.at[t, g, slot(0)], own_sem.at[t, g]
                )
            )

    def forward(t, g, d):
        ref = k_hbm if t == 0 else v_hbm
        src = ref.at[:, cols(first, g)] if d == 0 else win.at[t, g, slot(d)]
        return pltpu.make_async_remote_copy(
            src_ref=src,
            dst_ref=win.at[t, g, slot(d + 1)],
            send_sem=send_sem.at[t, g, d],
            recv_sem=recv_sem.at[t, g, d + 1],
            device_id={"ctx": up},
            device_id_type=MESH,
        )

    def forward_seg(d):
        return pltpu.make_async_remote_copy(
            src_ref=seg_hbm if d == 0 else segwin.at[d],
            dst_ref=segwin.at[d + 1],
            send_sem=seg_send.at[d],
            recv_sem=seg_recv.at[d + 1],
            device_id={"ctx": up},
            device_id_type=MESH,
        )

    pieces = [(t, r) for t in range(2) for r in range(halves)]

    def some(r):
        return pl.ds(r * HALF, HALF)

    def back(g, d, t, r):
        return pltpu.make_async_remote_copy(
            src_ref=sendb.at[g, d - 1, t, some(r)],
            dst_ref=ret.at[g, d - 1, t, some(r)],
            send_sem=back_send.at[g, d - 1, t, r],
            recv_sem=back_recv.at[g, d - 1, t, r],
            device_id={"ctx": down},
            device_id_type=MESH,
        )

    def owed(g, d, t, r):
        return acc[g, t, pl.ds((reach - d) * rows + r * HALF, HALF), :]

    def to_mate(g, t, r):
        return pltpu.make_async_remote_copy(
            src_ref=fin.at[g, t, some(r)],
            dst_ref=pfin.at[g, t, some(r)],
            send_sem=pair_send.at[g, t, r],
            recv_sem=pair_recv.at[g, t, r],
            device_id={"kv": mate},
            device_id_type=MESH,
        )

    has_up = rank < n - 1

    for copy in [seg_load] + owns + loads:
        copy.start()

    barrier = pltpu.get_barrier_semaphore()
    pl.semaphore_signal(barrier, inc=1, device_id={"kv": mate}, device_id_type=MESH)

    @pl.when(has_up)
    def _():
        pl.semaphore_signal(barrier, inc=1, device_id={"ctx": up}, device_id_type=MESH)

    @pl.when(rank > 0)
    def _():
        pl.semaphore_signal(barrier, inc=1, device_id={"ctx": down}, device_id_type=MESH)

    expected = 1 + jnp.where(has_up, 1, 0) + jnp.where(rank > 0, 1, 0)
    pl.semaphore_wait(barrier, expected)

    @pl.when(has_up)
    def _():
        forward_seg(0).start()
        forward(0, 0, 0).start()
        forward(1, 0, 0).start()

    for d in range(1, reach + 1):
        @pl.when(rank < d)
        def _(d=d):
            for g in range(kv_count):
                for t in range(2):
                    win[t, g, slot(d), :] = jnp.zeros((rows, HEAD_SIZE), jnp.bfloat16)
            segwin[d] = jnp.full((1, rows), -1, jnp.int32)

    acc[...] = jnp.zeros_like(acc)

    def pass_on_seg():
        for d in range(1, reach + 1):
            @pl.when(rank >= d)
            def _(d=d):
                forward_seg(d - 1).wait_recv()

            if d < reach:
                @pl.when((rank >= d) & has_up)
                def _(d=d):
                    forward_seg(d).start()

    def pass_on(g, kinds):
        for d in range(1, reach):
            for t in kinds:
                @pl.when(rank >= d)
                def _(d=d, t=t):
                    forward(t, g, d - 1).wait_recv()

                @pl.when((rank >= d) & has_up)
                def _(d=d, t=t):
                    forward(t, g, d).start()

    def last_slot(g):
        @pl.when(rank >= reach)
        def _():
            for t in range(2):
                forward(t, g, reach - 1).wait_recv()

    def send_own(g):
        @pl.when(has_up)
        def _():
            for t in range(2):
                forward(t, g, 0).start()

    def make_bias():
        for d in range(reach + 1):
            row = segwin[d].astype(jnp.float32)
            segcol[slot(d), :] = jnp.broadcast_to(row, (HALF, rows)).T
        key_at = lax.broadcasted_iota(jnp.int32, (width, HALF), 0)
        query_at = lax.broadcasted_iota(jnp.int32, (width, HALF), 1)
        causal = key_at <= query_at + reach * rows
        for h in range(halves):
            seg_q = segwin[0, :, h * HALF:(h + 1) * HALF].astype(jnp.float32)
            same = segcol[h * HALF:h * HALF + width, :] == seg_q
            bias[h] = jnp.where(same & causal, 0.0, NEG)

    def spot(g, h, p):
        c0 = pl.multiple_of((g * per_kv + 2 * p) * HEAD_SIZE, HEAD_SIZE)
        c1 = pl.multiple_of((g * per_kv + 2 * p + 1) * HEAD_SIZE, HEAD_SIZE)
        part = slice(h * HALF, (h + 1) * HALF)
        return part, pl.ds(c0, HEAD_SIZE), pl.ds(c1, HEAD_SIZE)

    def pair(ref, g, h, p):
        part, one, two = spot(g, h, p)
        return jnp.concatenate([ref[part, one], ref[part, two]], axis=0)

    def span(h):
        return slice(h * HALF, h * HALF + width)

    def products(g, h, p):
        s = lax.dot_general(
            win[0, g, span(h), :], pair(qv, g, h, p), NT, preferred_element_type=jnp.float32
        )
        b = bias[h]
        s = s + jnp.concatenate([b, b], axis=1)
        sv[h] = s
        peaks[h] = jnp.max(s, axis=0, keepdims=True)
        dpv[h] = lax.dot_general(
            win[1, g, span(h), :], pair(gv, g, h, p), NT, preferred_element_type=jnp.float32
        )

    def softmax(h):
        peak = peaks[h]
        total = jnp.zeros((8, 2 * HALF), jnp.float32)
        weighted = jnp.zeros((8, 2 * HALF), jnp.float32)
        for c in range(0, width, CHUNK):
            rows_c = slice(c, c + CHUNK)
            e = jnp.exp2((sv[h, rows_c, :] - peak) * (scale * LOG2E))
            sv[h, rows_c, :] = e
            total = total + jnp.sum(e.reshape(-1, 8, 2 * HALF), axis=0)
            weighted = weighted + jnp.sum(
                (e * dpv[h, rows_c, :]).reshape(-1, 8, 2 * HALF), axis=0
            )
        inv = 1.0 / jnp.sum(total, axis=0, keepdims=True)
        delta = jnp.sum(weighted, axis=0, keepdims=True) * inv
        for c in range(0, width, CHUNK):
            rows_c = slice(c, c + CHUNK)
            pn = sv[h, rows_c, :] * inv
            dsv[h, rows_c, :] = (pn * (dpv[h, rows_c, :] - delta)).astype(jnp.bfloat16)
            pv[h, rows_c, :] = pn.astype(jnp.bfloat16)

    def grads(g, h, p):
        part, one, two = spot(g, h, p)
        ds = dsv[h]
        dqt = jnp.dot(kt[g, :, span(h)], ds, preferred_element_type=jnp.float32)
        dq = (dqt * scale).T.astype(jnp.bfloat16)
        dqv[part, one] = dq[:HALF]
        dqv[part, two] = dq[HALF:]
        acc[g, 0, span(h), :] += jnp.dot(
            ds, pair(qv, g, h, p), preferred_element_type=jnp.float32
        )
        acc[g, 1, span(h), :] += jnp.dot(
            pv[h], pair(gv, g, h, p), preferred_element_type=jnp.float32
        )

    pairs = per_kv // 2
    last_half = halves - 1

    def begin_units(g):
        dsv[last_half] = jnp.zeros((width, 2 * HALF), jnp.bfloat16)
        pv[last_half] = jnp.zeros((width, 2 * HALF), jnp.bfloat16)
        products(g, 0, 0)

    def units(g, begin, end):
        def body(p, carry):
            for h in range(halves):
                if h < last_half:
                    products(g, h + 1, p)
                else:
                    products(g, 0, jnp.minimum(p + 1, pairs - 1))
                softmax(h)
                if h > 0:
                    grads(g, h - 1, p)
                else:
                    grads(g, last_half, jnp.maximum(p - 1, 0))
            return carry

        lax.fori_loop(begin, end, body, 0)

    def end_units(g):
        grads(g, last_half, pairs - 1)

    def send_first(g):
        for d in range(reach, 0, -1):
            @pl.when((rank >= d) if d == reach else jnp.logical_not(has_up))
            def _(d=d):
                for t, r in pieces:
                    sendb[g, d - 1, t, some(r), :] = owed(g, d, t, r).astype(jnp.bfloat16)
                    back(g, d, t, r).start()

    def send_rest(g):
        for d in range(reach - 1, 0, -1):
            @pl.when(has_up & (rank >= d))
            def _(d=d):
                for t, r in pieces:
                    back(g, d + 1, t, r).wait_recv()
                    sendb[g, d - 1, t, some(r), :] = (
                        owed(g, d, t, r) + ret[g, d, t, some(r), :].astype(jnp.float32)
                    ).astype(jnp.bfloat16)
                    back(g, d, t, r).start()

    def finish(g):
        for t, r in pieces:
            @pl.when(has_up)
            def _(t=t, r=r):
                back(g, 1, t, r).wait_recv()
                acc[g, t, pl.ds(reach * rows + r * HALF, HALF), :] += (
                    ret[g, 0, t, some(r), :].astype(jnp.float32)
                )

            factor = scale if t == 0 else 1.0
            fin[g, t, some(r), :] = (owed(g, 0, t, r) * factor).astype(jnp.bfloat16)
            to_mate(g, t, r).start()

    pass_on_seg()
    seg_load.wait()
    make_bias()
    pass_on(0, (0, 1))
    for copy in loads + owns:
        copy.wait()
    early, middle, late = pairs // 4, pairs // 2, pairs * 3 // 4
    for g in range(kv_count):
        if g + 1 < kv_count:
            send_own(g + 1)
        last_slot(g)
        kt[g] = win[0, g].T
        begin_units(g)
        if g + 1 < kv_count:
            units(g, 0, early)
            pass_on(g + 1, (0,))
            units(g, early, middle)
            pass_on(g + 1, (1,))
            if g > 0:
                send_rest(g - 1)
            units(g, middle, pairs)
        elif g > 0:
            units(g, 0, late)
            send_rest(g - 1)
            units(g, late, pairs)
        else:
            units(g, 0, pairs)
        end_units(g)
        send_first(g)
    send_rest(kv_count - 1)
    for g in range(kv_count):
        finish(g)

    for g in range(kv_count):
        for t in range(2):
            for r in range(halves):
                to_mate(g, t, r).wait()
            if shared:
                other[g, t] = (
                    fin[g, t].astype(jnp.float32) + pfin[g, t].astype(jnp.float32)
                ).astype(jnp.bfloat16)
            else:
                other[g, t] = pfin[g, t]
    for d in range(reach):
        @pl.when(has_up & (rank >= d))
        def _(d=d):
            forward_seg(d).wait_send()
            for g in range(kv_count):
                for t in range(2):
                    forward(t, g, d).wait_send()
    for d in range(1, reach + 1):
        @pl.when(rank >= d)
        def _(d=d):
            for g in range(kv_count):
                for t, r in pieces:
                    back(g, d, t, r).wait_send()


def place(kv_count, shared, dqv, fin, other, dq_hbm, dk_hbm, dv_hbm, sem):
    kv = lax.axis_index("kv")
    copies = [pltpu.make_async_copy(dqv, dq_hbm, sem.at[0])]
    parts = [(other, 0)] if shared else [(fin, kv * kv_count), (other, (1 - kv) * kv_count)]
    for source, base in parts:
        for g in range(kv_count):
            start = g * HEAD_SIZE
            if not shared:
                start = pl.multiple_of((base + g) * HEAD_SIZE, HEAD_SIZE)
            for t, ref in ((0, dk_hbm), (1, dv_hbm)):
                copies.append(
                    pltpu.make_async_copy(
                        source.at[g, t], ref.at[:, pl.ds(start, HEAD_SIZE)], sem.at[len(copies)]
                    )
                )
    for copy in copies:
        copy.start()
    for copy in copies:
        copy.wait()


def shards(queries, key_matrix, value_matrix, out_grad, segments):
    n = lax.axis_size("ctx")
    rows = queries.shape[0]
    head_count = queries.shape[1] // HEAD_SIZE
    group_width = QUERY_HEADS // KEY_VALUE_HEADS
    kv_count = max(head_count // group_width, 1)
    per_kv = head_count // kv_count
    kv_here = key_matrix.shape[1] // HEAD_SIZE
    shared = kv_here < kv_count * lax.axis_size("kv")
    reach = n // 2
    window = (reach + 1) * rows
    width = reach * rows + HALF
    halves = rows // HALF
    bf16, f32 = jnp.bfloat16, jnp.float32
    dma = pltpu.SemaphoreType.DMA
    anywhere = pl.BlockSpec(memory_space=pltpu.HBM)
    inner = pltpu.VMEM
    dqv, fin, other = pl.pallas_call(
        functools.partial(kernel, n, reach, rows, per_kv, kv_count, shared),
        out_shape=(
            inner(queries.shape, bf16),
            inner((kv_count, 2, rows, HEAD_SIZE), bf16),
            inner((kv_count, 2, rows, HEAD_SIZE), bf16),
        ),
        in_specs=[anywhere] * 5,
        out_specs=(pl.BlockSpec(memory_space=pltpu.VMEM),) * 3,
        scratch_shapes=[
            pltpu.VMEM(queries.shape, bf16),
            pltpu.VMEM(queries.shape, bf16),
            pltpu.VMEM((halves, width, 2 * HALF), f32),
            pltpu.VMEM((halves, width, 2 * HALF), f32),
            pltpu.VMEM((halves, 1, 2 * HALF), f32),
            pltpu.VMEM((halves, width, 2 * HALF), bf16),
            pltpu.VMEM((halves, width, 2 * HALF), bf16),
            pltpu.VMEM((2, kv_count, window, HEAD_SIZE), bf16),
            pltpu.VMEM((reach + 1, 1, rows), jnp.int32),
            pltpu.VMEM((window, HALF), f32),
            pltpu.VMEM((halves, width, HALF), f32),
            pltpu.VMEM((kv_count, HEAD_SIZE, window), bf16),
            pltpu.VMEM((kv_count, 2, window, HEAD_SIZE), f32),
            pltpu.VMEM((kv_count, reach, 2, rows, HEAD_SIZE), bf16),
            pltpu.VMEM((kv_count, reach, 2, rows, HEAD_SIZE), bf16),
            pltpu.VMEM((kv_count, 2, rows, HEAD_SIZE), bf16),
            dma((3,)),
            dma((2, kv_count)),
            dma((reach + 1,)),
            dma((reach + 1,)),
            dma((2, kv_count, reach + 1)),
            dma((2, kv_count, reach + 1)),
            dma((kv_count, reach, 2, halves)),
            dma((kv_count, reach, 2, halves)),
            dma((kv_count, 2, halves)),
            dma((kv_count, 2, halves)),
        ],
        compiler_params=pltpu.CompilerParams(
            collective_id=0, has_side_effects=True, vmem_limit_bytes=56 * 1024 * 1024
        ),
    )(queries, key_matrix, value_matrix, out_grad, segments.reshape(1, rows))
    return pl.pallas_call(
        functools.partial(place, kv_count, shared),
        out_shape=(
            jax.ShapeDtypeStruct(queries.shape, bf16),
            jax.ShapeDtypeStruct(key_matrix.shape, bf16),
            jax.ShapeDtypeStruct(value_matrix.shape, bf16),
        ),
        in_specs=[pl.BlockSpec(memory_space=pltpu.VMEM)] * 3,
        out_specs=(anywhere,) * 3,
        scratch_shapes=[dma((1 + 4 * kv_count,))],
        compiler_params=pltpu.CompilerParams(vmem_limit_bytes=4 * 1024 * 1024),
    )(dqv, fin, other)


def solution(mesh):
    return jax.shard_map(
        shards,
        mesh=mesh,
        in_specs=(
            P(("groups", "ctx"), ("tp", "kv")),
            P(("groups", "ctx"), "tp"),
            P(("groups", "ctx"), "tp"),
            P(("groups", "ctx"), ("tp", "kv")),
            P(("groups", "ctx")),
        ),
        out_specs=(
            P(("groups", "ctx"), ("tp", "kv")),
            P(("groups", "ctx"), "tp"),
            P(("groups", "ctx"), "tp"),
        ),
        check_vma=False,
    )
```
